512 devices in a mesh: row: 16 (over y, core), col: 32 (over z, x).
Axes of the slice: x: 4, y: 8, z: 8, core: 2. Of those that a mesh axis runs over, the one named last changes fastest.
Arguments:
- child_vectors: bfloat16 [2, 8192, 65536], P(None, 'row', 'col'), may hold values from -6 to 6
- merge_position: int32 [2, 65536], P(None, 'col'), may hold values from 0 to 131071, as said below
- pole_frac: float32 [2, 65536], P(None, 'col'), may hold values from 0 to 0.3
- weights: float32 [2, 65536], P(None, 'col'), may hold values from -3 to 3, as said below
- retained: int32 [2, 65536], P(None, 'col'), may hold values from 0 to 1, as said below
- root_index: int32 [512], replicated, may hold values from 0 to 131070
- root_offset: float32 [512], replicated, may hold values from 0.55 to 0.75
Outputs:
- merged: bfloat16 [2, 8192, 512], P(None, ('row', 'col'))
The draws below stay inside these ranges and needn't reach their ends.
Inputs may be any that keep to these rules, and one draw needn't show every extreme that they name: `merge_position`: each merged position 0 to 131071 occurs exactly once over both children. The first pole of each aligned block of 2048 poles of a child is retained; elsewhere whole aligned blocks of 512 poles may be deflated. `weights`: magnitudes lie between 0.3 and 3.
All inputs are finite; a program needn't handle non-finite values.
Results may differ from the reference program's by a relative error of at most 0.015.
Values may be sent and summed in bfloat16 or wider, within the bound.
A program may use at most 64 MiB of HBM per device.

```python
import math
import jax
import jax.numpy as jnp
from jax import lax

HALF_DEV = 2048
TILE = 512
HALF = 65536
ORDER = 131072
ROWS = 8192
COLS = 512
N_COL = 32


def draw_merge_position(key, part):
    order_values = jax.random.permutation(jax.random.fold_in(key, 11), jnp.arange(ORDER, dtype=jnp.int32))
    return order_values.reshape(2, HALF).astype(jnp.int32)


def draw_weights(key, part):
    sign_key = jax.random.fold_in(key, 21)
    size_key = jax.random.fold_in(key, 22)
    signs = jnp.where(jax.random.bernoulli(sign_key, 0.5, (2, HALF)), 1.0, -1.0)
    magnitude = jnp.exp(jax.random.uniform(size_key, (2, HALF), jnp.float32, math.log(0.3), math.log(3.0)))
    return (signs * magnitude).astype(jnp.float32)


def draw_retained(key, part):
    levels = jax.random.randint(jax.random.fold_in(key, 31), (2, HALF // TILE), 0, 5)
    coins = jax.random.randint(jax.random.fold_in(key, 32), (2, HALF), 0, 4)
    thresholds = jnp.repeat(levels, TILE, axis=1)
    leading = (jnp.arange(HALF) % HALF_DEV == 0)[None, :]
    return jnp.logical_or(coins < thresholds, leading).astype(jnp.int32)


def with_ends(result, own_key, smallest, top_value):
    longest = result.shape.index(max(result.shape))
    spots = []
    for shift in (0, 1):
        where = [jax.random.randint(jax.random.fold_in(own_key, axis), (), 0, length) for axis, length in enumerate(result.shape)]
        where[longest] = (where[longest] + shift) % result.shape[longest]
        spots.append(tuple(where))
    return result.at[spots[0]].set(smallest).at[spots[1]].set(top_value)


def block_scale(stream_key, shape, cuts, smallest, high):
    def one(position, blocks):
        draws = jax.random.uniform(jax.random.fold_in(jax.random.fold_in(stream_key, 6), position), (blocks,), jnp.float32, smallest / len(cuts), high / len(cuts))
        return jnp.repeat(jnp.exp(draws), shape[position] // blocks).reshape((-1,) + (1,) * (len(shape) - position - 1))

    gain = one(*cuts[0])
    for cut in cuts[1:]:
        gain = gain * one(*cut)
    return gain


def normal_values(stream_key, extent, scale, most, cuts=(), held_as=jnp.bfloat16):
    entries = jax.random.normal(stream_key, extent, jnp.float32) * scale
    if len(cuts) > 0:
        entries = block_scale(stream_key, extent, cuts, -0.22, 0.18) * entries
    return jnp.clip(entries, min=-most, max=most).astype(held_as)


def setup_inputs(seed: int = 0) -> dict:
    seeds = jax.random.split(jax.random.key(seed), 8)
    return {
        "child_vectors": normal_values(seeds[0], (2, ROWS, HALF), 1.0, 6.0, ((1, 16), (2, 32))),
        "merge_position": draw_merge_position(jax.random.fold_in(seeds[7], 71), 0),
        "pole_frac": jnp.clip(0.3 * jax.random.uniform(seeds[2], (2, HALF), jnp.float32) ** block_scale(seeds[2], (2, HALF), ((1, 32),), -0.2, 0.2), 0.0, 0.3),
        "weights": draw_weights(jax.random.fold_in(seeds[7], 71), 0),
        "retained": draw_retained(jax.random.fold_in(seeds[7], 71), 0),
        "root_index": with_ends(jax.random.randint(seeds[5], (COLS,), 0, ORDER - 1), jax.random.fold_in(seeds[5], 1), 0, (ORDER - 1) - 1).astype(jnp.int32),
        "root_offset": jnp.clip(jax.random.uniform(seeds[6], (COLS,), jnp.float32, 0.55, 0.75), 0.55, 0.75),
    }


def reference(child_vectors, merge_position, pole_frac, weights, retained, root_index, root_offset):
    spacing = (merge_position[:, :, None] - root_index[None, None, :]).astype(jnp.float32) + (pole_frac[:, :, None] - root_offset[None, None, :])
    raw_panel = (retained.astype(jnp.float32) * weights)[:, :, None] / spacing
    totals = lax.optimization_barrier(jnp.sum(raw_panel * raw_panel, axis=(0, 1)))
    panel_block = (raw_panel * lax.rsqrt(totals)[None, None, :]).astype(jnp.bfloat16)

    def add_block(running, number):
        first_col = (number * HALF_DEV).astype(jnp.int32)
        vector_block = lax.dynamic_slice_in_dim(child_vectors, first_col, HALF_DEV, 2).astype(jnp.float32)
        panel_part = lax.dynamic_slice_in_dim(panel_block, first_col, HALF_DEV, 1).astype(jnp.float32)
        partial_value = jnp.einsum('crh,chm->crm', vector_block, panel_part)
        rounded = lax.optimization_barrier(partial_value.astype(jnp.bfloat16)).astype(jnp.float32)
        return (running + rounded, None)
    running, unused = lax.scan(add_block, jnp.zeros((2, ROWS, COLS), jnp.float32), jnp.arange(N_COL, dtype=jnp.int32))
    return running.astype(jnp.bfloat16)
```

```python
import jax
import jax.numpy as jnp
from jax import lax
from jax.experimental import pallas as pl
from jax.experimental.pallas import tpu as pltpu
from jax.sharding import PartitionSpec as P

NX = 4
NZ = 8
MESH = pl.DeviceIdType.MESH
STAGES = ((0, 0), (1, 0), (0, 1), (1, 1))
WIDTH = 256


def kernel(
    vectors_hbm,
    position_ref,
    fraction_ref,
    weight_ref,
    keep_ref,
    root_ref,
    offset_ref,
    out_ref,
    vectors,
    panel,
    poles,
    roots,
    squares,
    part,
    ring,
    sent,
    arrived,
    spread,
    landed,
    own_total,
    x_totals,
    z_own,
    z_totals,
    load_sem,
    x_send,
    x_recv,
    z_send,
    z_recv,
    tx_send,
    tx_recv,
    tz_send,
    tz_recv,
):
    col = lax.axis_index("col")
    z = col // NX
    x = col % NX

    def at(zz, xx):
        return {"col": zz * NX + xx}

    right = (x + 1) % NX
    left = (x + NX - 1) % NX
    across = (x + 2) % NX
    z_peers = [(z + d) % NZ for d in (4, 3, 5, 2, 6, 1, 7)]

    barrier = pltpu.get_barrier_semaphore()
    for xx in (right, left, across):
        pl.semaphore_signal(barrier, inc=1, device_id=at(z, xx), device_id_type=MESH)
    for zz in z_peers:
        pl.semaphore_signal(barrier, inc=1, device_id=at(zz, x), device_id_type=MESH)

    loads = []
    for child in range(2):
        copies = []
        for xx in range(NX):
            copy = pltpu.make_async_copy(
                vectors_hbm.at[child, :, xx], vectors.at[child, xx], load_sem.at[child, xx]
            )
            copy.start()
            copies.append(copy)
        loads.append(copies)

    half = position_ref.shape[1]
    for child in range(2):
        row = slice(child, child + 1)
        poles[child, 0] = jnp.broadcast_to(position_ref[row, :].astype(jnp.float32), (8, half))
        poles[child, 1] = jnp.broadcast_to(fraction_ref[row, :], (8, half))
        poles[child, 2] = jnp.broadcast_to(
            keep_ref[row, :].astype(jnp.float32) * weight_ref[row, :], (8, half)
        )
    for block in range(4):
        lanes = slice(block * 128, block * 128 + 128)
        roots[0, block * 16 : block * 16 + 16] = jnp.broadcast_to(
            root_ref[:, lanes].astype(jnp.float32), (128, 128)
        ).T.reshape(16, 8, 128)
        roots[1, block * 16 : block * 16 + 16] = jnp.broadcast_to(
            offset_ref[:, lanes], (128, 128)
        ).T.reshape(16, 8, 128)

    def make_panel(child, side):
        def body(step, carry):
            first = side * 32 + step * 4
            root_rows = roots[0, pl.ds(first, 4)]
            offset_rows = roots[1, pl.ds(first, 4)]
            total = jnp.zeros((4, 8, 128), jnp.float32)
            for block in range(half // 128):
                lanes = slice(block * 128, block * 128 + 128)
                spacing = (poles[child, 0, :, lanes][None] - root_rows) + (
                    poles[child, 1, :, lanes][None] - offset_rows
                )
                raw = poles[child, 2, :, lanes][None] / spacing
                total = total + raw * raw
                panel[child, pl.ds(pl.multiple_of(first * 8, 32), 32), lanes] = raw.reshape(
                    32, 128
                ).astype(jnp.bfloat16)
            if child == 0:
                squares[pl.ds(first, 4)] = total
            else:
                squares[pl.ds(first, 4)] = squares[pl.ds(first, 4)] + total
            return carry

        lax.fori_loop(0, 8, body, 0)

    def remote(src, dst, send, recv, target):
        return pltpu.make_async_remote_copy(
            src_ref=src, dst_ref=dst, send_sem=send, recv_sem=recv, device_id=target, device_id_type=MESH
        )

    upper, lower = pl.ds(0, 4), pl.ds(4, 4)
    x_copies = {}
    z_copies = {}

    def send_first(s):
        for d, (near, far, near_half, far_half) in enumerate(
            ((right, across, lower, upper), (left, across, upper, lower))
        ):
            x_copies[s, d, 0] = remote(
                part.at[s, far, far_half],
                ring.at[s, d],
                x_send.at[s, d, 0],
                x_recv.at[s, d, 0],
                at(z, near),
            )
            x_copies[s, d, 1] = remote(
                part.at[s, near, near_half],
                arrived.at[s, d, near_half],
                x_send.at[s, d, 1],
                x_recv.at[s, d, 1],
                at(z, near),
            )
            x_copies[s, d, 0].start()
            x_copies[s, d, 1].start()

    def send_second(s):
        for d, (near, half_rows) in enumerate(((right, upper), (left, lower))):
            x_copies[s, d, 0].wait_recv()
            sent[s, d] = (
                part[s, near, half_rows].astype(jnp.float32) + ring[s, d].astype(jnp.float32)
            ).astype(jnp.bfloat16)
            x_copies[s, d, 2] = remote(
                sent.at[s, d],
                arrived.at[s, d, half_rows],
                x_send.at[s, d, 2],
                x_recv.at[s, d, 2],
                at(z, near),
            )
            x_copies[s, d, 2].start()

    def send_third(s):
        for d in range(2):
            x_copies[s, d, 1].wait_recv()
            x_copies[s, d, 2].wait_recv()
        spread[s] = (
            part[s, x].astype(jnp.float32)
            + arrived[s, 0].astype(jnp.float32)
            + arrived[s, 1].astype(jnp.float32)
        ).astype(jnp.bfloat16)
        for n, zz in enumerate(z_peers):
            z_copies[s, n] = remote(
                spread.at[s, zz], landed.at[s, n], z_send.at[s, n], z_recv.at[s, n], at(zz, x)
            )
            z_copies[s, n].start()

    for s, (child, side) in enumerate(STAGES):
        make_panel(child, side)
        if side == 0:
            for copy in loads[child]:
                copy.wait()
        block = lax.dot_general(
            vectors[child].reshape(NX * NZ * 16, half),
            panel[child, side * WIDTH : side * WIDTH + WIDTH, :],
            (((1,), (1,)), ((), ())),
            preferred_element_type=jnp.float32,
        )
        part[s] = block.astype(jnp.bfloat16).reshape(NX, NZ, 16, WIDTH)
        if s == 0:
            pl.semaphore_wait(barrier, NX - 1 + NZ - 1)
        send_first(s)
        if s >= 1:
            send_second(s - 1)
        if s >= 2:
            send_third(s - 2)

    for block in range(4):
        own_total[:, block * 128 : block * 128 + 128] = jnp.broadcast_to(
            jnp.sum(squares[block * 16 : block * 16 + 16].reshape(128, 128).T, axis=0, keepdims=True),
            (8, 128),
        )
    tx_copies = []
    for n, xx in enumerate((across, right, left)):
        copy = remote(own_total, x_totals.at[n], tx_send.at[n], tx_recv.at[n], at(z, xx))
        copy.start()
        tx_copies.append(copy)

    last = len(STAGES) - 1
    send_second(last)
    send_third(last - 1)
    for copy in tx_copies:
        copy.wait_recv()
    z_own[...] = own_total[...] + x_totals[0] + x_totals[1] + x_totals[2]
    tz_copies = []
    for n, zz in enumerate(z_peers):
        copy = remote(z_own, z_totals.at[n], tz_send.at[n], tz_recv.at[n], at(zz, x))
        copy.start()
        tz_copies.append(copy)
    send_third(last)

    total = z_own[...]
    for n, copy in enumerate(tz_copies):
        copy.wait_recv()
        total = total + z_totals[n]
    scale = lax.rsqrt(total)
    for s, (child, side) in enumerate(STAGES):
        result = spread[s, z].astype(jnp.float32)
        for n in range(len(z_peers)):
            z_copies[s, n].wait_recv()
            result = result + landed[s, n].astype(jnp.float32)
        lanes = slice(side * WIDTH, side * WIDTH + WIDTH)
        out_ref[child, :, lanes] = (result * scale[0:1, lanes]).astype(jnp.bfloat16)

    for copy in list(x_copies.values()) + list(z_copies.values()) + tx_copies + tz_copies:
        copy.wait_send()


def local(child_vectors, merge_position, pole_frac, weights, retained, root_index, root_offset):
    children, rows, half = child_vectors.shape
    cols = root_index.shape[0]
    stages = len(STAGES)
    bf16, f32 = jnp.bfloat16, jnp.float32
    dma = pltpu.SemaphoreType.DMA
    vmem = pl.BlockSpec(memory_space=pltpu.VMEM)
    return pl.pallas_call(
        kernel,
        out_shape=jax.ShapeDtypeStruct((children, 16, cols), bf16),
        in_specs=[pl.BlockSpec(memory_space=pl.ANY)] + [vmem] * 6,
        out_specs=vmem,
        scratch_shapes=[
            pltpu.VMEM((children, NX, NZ, 16, half), bf16),
            pltpu.VMEM((children, cols, half), bf16),
            pltpu.VMEM((children, 3, 8, half), f32),
            pltpu.VMEM((2, cols // 8, 8, 128), f32),
            pltpu.VMEM((cols // 8, 8, 128), f32),
            pltpu.VMEM((stages, NX, NZ, 16, WIDTH), bf16),
            pltpu.VMEM((stages, 2, NZ // 2, 16, WIDTH), bf16),
            pltpu.VMEM((stages, 2, NZ // 2, 16, WIDTH), bf16),
            pltpu.VMEM((stages, 2, NZ, 16, WIDTH), bf16),
            pltpu.VMEM((stages, NZ, 16, WIDTH), bf16),
            pltpu.VMEM((stages, NZ - 1, 16, WIDTH), bf16),
            pltpu.VMEM((8, cols), f32),
            pltpu.VMEM((NX - 1, 8, cols), f32),
            pltpu.VMEM((8, cols), f32),
            pltpu.VMEM((NZ - 1, 8, cols), f32),
            dma((children, NX)),
            dma((stages, 2, 3)),
            dma((stages, 2, 3)),
            dma((stages, NZ - 1)),
            dma((stages, NZ - 1)),
            dma((NX - 1,)),
            dma((NX - 1,)),
            dma((NZ - 1,)),
            dma((NZ - 1,)),
        ],
        compiler_params=pltpu.CompilerParams(collective_id=0, has_side_effects=True),
        name="panel_product",
    )(
        child_vectors.reshape(children, NZ, NX, 16, half),
        merge_position,
        pole_frac,
        weights,
        retained,
        root_index.reshape(1, cols),
        root_offset.reshape(1, cols),
    )


def solution(mesh):
    return jax.shard_map(
        local,
        mesh=mesh,
        in_specs=(
            P(None, "row", "col"),
            P(None, "col"),
            P(None, "col"),
            P(None, "col"),
            P(None, "col"),
            P(),
            P(),
        ),
        out_specs=P(None, ("row", "col"), None),
        check_vma=False,
    )
```

```python
import jax
import jax.numpy as jnp
from jax import lax
from jax.experimental import pallas as pl
from jax.experimental.pallas import tpu as pltpu
from jax.sharding import PartitionSpec as P

NX = 4
NZ = 8
MESH = pl.DeviceIdType.MESH
OWNERS = NZ // 2
WIDTH = 256


def kernel(
    vectors_hbm,
    position_hbm,
    fraction_hbm,
    weight_hbm,
    keep_hbm,
    root_hbm,
    offset_hbm,
    out_ref,
    position_ref,
    fraction_ref,
    weight_ref,
    keep_ref,
    root_ref,
    offset_ref,
    vectors,
    panel,
    poles,
    roots,
    squares,
    part,
    arrived,
    spread,
    landed,
    own_total,
    x_totals,
    z_own,
    z_totals,
    small_sem,
    load_sem,
    x_send,
    x_recv,
    z_send,
    z_recv,
    tx_send,
    tx_recv,
    tz_send,
    tz_recv,
):
    small = []
    for n, (source, target) in enumerate(
        (
            (root_hbm, root_ref),
            (offset_hbm, offset_ref),
            (position_hbm, position_ref),
            (fraction_hbm, fraction_ref),
            (weight_hbm, weight_ref),
            (keep_hbm, keep_ref),
        )
    ):
        copy = pltpu.make_async_copy(source, target, small_sem.at[n])
        copy.start()
        small.append(copy)

    col = lax.axis_index("col")
    z = col // NX
    x = col % NX

    def at(zz, xx):
        return {"col": zz * NX + xx}

    x_peers = [(x + d) % NX for d in (2, 1, 3)]
    z_peers = [(z + d) % NZ for d in (4, 3, 5, 2, 6, 1, 7)]

    barrier = pltpu.get_barrier_semaphore()
    for xx in x_peers:
        pl.semaphore_signal(barrier, inc=1, device_id=at(z, xx), device_id_type=MESH)
    for zz in z_peers:
        pl.semaphore_signal(barrier, inc=1, device_id=at(zz, x), device_id_type=MESH)

    loads = {}
    for child in range(2):
        for group in range(2):
            owners = pl.ds(group * OWNERS, OWNERS)
            loads[group, child] = []
            for xx in range(NX):
                copy = pltpu.make_async_copy(
                    vectors_hbm.at[child, owners, xx],
                    vectors.at[group, child, xx],
                    load_sem.at[group, child, xx],
                )
                copy.start()
                loads[group, child].append(copy)

    for copy in small:
        copy.wait()

    half = position_ref.shape[1]
    for child in range(2):
        row = slice(child, child + 1)
        poles[child, 0] = jnp.broadcast_to(position_ref[row, :].astype(jnp.float32), (8, half))
        poles[child, 1] = jnp.broadcast_to(fraction_ref[row, :], (8, half))
        poles[child, 2] = jnp.broadcast_to(
            keep_ref[row, :].astype(jnp.float32) * weight_ref[row, :], (8, half)
        )
    for block in range(4):
        lanes = slice(block * 128, block * 128 + 128)
        roots[0, block * 16 : block * 16 + 16] = jnp.broadcast_to(
            root_ref[:, lanes].astype(jnp.float32), (128, 128)
        ).T.reshape(16, 8, 128)
        roots[1, block * 16 : block * 16 + 16] = jnp.broadcast_to(
            offset_ref[:, lanes], (128, 128)
        ).T.reshape(16, 8, 128)

    def make_panel(child, side):
        def body(step, carry):
            first = side * 32 + step * 4
            root_rows = roots[0, pl.ds(first, 4)]
            offset_rows = roots[1, pl.ds(first, 4)]
            total = jnp.zeros((4, 8, 128), jnp.float32)
            for block in range(half // 128):
                lanes = slice(block * 128, block * 128 + 128)
                spacing = (poles[child, 0, :, lanes][None] - root_rows) + (
                    poles[child, 1, :, lanes][None] - offset_rows
                )
                raw = poles[child, 2, :, lanes][None] / spacing
                total = total + raw * raw
                panel[child, pl.ds(pl.multiple_of(first * 8, 32), 32), lanes] = raw.reshape(
                    32, 128
                ).astype(jnp.bfloat16)
            if child == 0:
                squares[pl.ds(first, 4)] = total
            else:
                squares[pl.ds(first, 4)] = squares[pl.ds(first, 4)] + total
            return carry

        lax.fori_loop(0, 8, body, 0)

    def remote(src, dst, send, recv, target):
        return pltpu.make_async_remote_copy(
            src_ref=src, dst_ref=dst, send_sem=send, recv_sem=recv, device_id=target, device_id_type=MESH
        )

    x_copies = {}
    z_copies = {}

    def multiply(group, child, first, count):
        columns = slice(first * WIDTH, (first + count) * WIDTH)
        block = lax.dot_general(
            vectors[group, child].reshape(NX * OWNERS * 16, half),
            panel[child, columns],
            (((1,), (1,)), ((), ())),
            preferred_element_type=jnp.float32,
        ).astype(jnp.bfloat16)
        for n in range(count):
            part[group, child, first + n] = block[:, n * WIDTH : n * WIDTH + WIDTH].reshape(NX, OWNERS, 16, WIDTH)

    def send_x(group, child, side):
        unit = (group, child, side)
        for n, xx in enumerate(x_peers):
            copy = remote(
                part.at[group, child, side, xx],
                arrived.at[group, child, side, n],
                x_send.at[group, child, side, n],
                x_recv.at[group, child, side, n],
                at(z, xx),
            )
            copy.start()
            x_copies[unit + (n,)] = copy

    def z_copy(child, side, n):
        return remote(
            spread.at[child, side, z_peers[n]],
            landed.at[child, side, n],
            z_send.at[child, side, n],
            z_recv.at[child, side, n],
            at(z_peers[n], x),
        )

    def send_z(group, child, side):
        total = part[group, child, side, x].astype(jnp.float32)
        for n in range(NX - 1):
            x_copies[group, child, side, n].wait_recv()
            total = total + arrived[group, child, side, n].astype(jnp.float32)
        spread[child, side, group * OWNERS : (group + 1) * OWNERS] = total.astype(jnp.bfloat16)
        for n, zz in enumerate(z_peers):

            @pl.when(zz // OWNERS == group)
            def _(n=n):
                z_copy(child, side, n).start()

    tx_copies = []
    for child in range(2):
        for side in range(2):
            make_panel(child, side)
            if child == 1:
                for block in range(2 * side, 2 * side + 2):
                    own_total[block : block + 1] = jnp.sum(
                        squares[block * 16 : block * 16 + 16].reshape(128, 128).T, axis=0, keepdims=True
                    )
            if side == 0:
                for copy in loads[0, child]:
                    copy.wait()
            multiply(0, child, side, 1)
            if (child, side) == (0, 0):
                pl.semaphore_wait(barrier, NX - 1 + NZ - 1)
            if (child, side) == (1, 1):
                for n, xx in enumerate(x_peers):
                    copy = remote(own_total, x_totals.at[n], tx_send.at[n], tx_recv.at[n], at(z, xx))
                    copy.start()
                    tx_copies.append(copy)
            send_x(0, child, side)

    for child in range(2):
        for copy in loads[1, child]:
            copy.wait()
        multiply(1, child, 0, 2)
        send_x(1, child, 0)
        send_x(1, child, 1)
        send_z(0, 0, child)

    send_z(0, 1, 0)
    for copy in tx_copies:
        copy.wait_recv()
    z_own[...] = own_total[...] + x_totals[0] + x_totals[1] + x_totals[2]
    tz_copies = []
    for n, zz in enumerate(z_peers):
        copy = remote(z_own, z_totals.at[n], tz_send.at[n], tz_recv.at[n], at(zz, x))
        copy.start()
        tz_copies.append(copy)
    send_z(0, 1, 1)
    for child in range(2):
        for side in range(2):
            send_z(1, child, side)

    total = z_own[...]
    for n, copy in enumerate(tz_copies):
        copy.wait_recv()
        total = total + z_totals[n]
    scale = lax.rsqrt(total)
    for child in range(2):
        for side in range(2):
            result = spread[child, side, z].astype(jnp.float32)
            for n in range(NZ - 1):
                z_copy(child, side, n).wait_recv()
                result = result + landed[child, side, n].astype(jnp.float32)
            for block in range(2 * side, 2 * side + 2):
                lanes = slice(block * 128 - side * WIDTH, block * 128 - side * WIDTH + 128)
                out_ref[child, :, block * 128 : block * 128 + 128] = (
                    result[:, lanes] * scale[block : block + 1]
                ).astype(jnp.bfloat16)

    for child in range(2):
        for side in range(2):
            for n in range(NZ - 1):
                z_copy(child, side, n).wait_send()
    for copy in list(x_copies.values()) + tx_copies + tz_copies:
        copy.wait_send()


def local(child_vectors, merge_position, pole_frac, weights, retained, root_index, root_offset):
    children, rows, half = child_vectors.shape
    cols = root_index.shape[0]
    bf16, f32 = jnp.bfloat16, jnp.float32
    dma = pltpu.SemaphoreType.DMA
    sides = cols // WIDTH
    return pl.pallas_call(
        kernel,
        out_shape=jax.ShapeDtypeStruct((children, 16, cols), bf16),
        in_specs=[pl.BlockSpec(memory_space=pltpu.HBM)] * 7,
        out_specs=pl.BlockSpec(memory_space=pltpu.VMEM),
        scratch_shapes=[
            pltpu.VMEM((children, half), jnp.int32),
            pltpu.VMEM((children, half), f32),
            pltpu.VMEM((children, half), f32),
            pltpu.VMEM((children, half), jnp.int32),
            pltpu.VMEM((1, cols), jnp.int32),
            pltpu.VMEM((1, cols), f32),
            pltpu.VMEM((2, children, NX, OWNERS, 16, half), bf16),
            pltpu.VMEM((children, cols, half), bf16),
            pltpu.VMEM((children, 3, 8, half), f32),
            pltpu.VMEM((2, cols // 8, 8, 128), f32),
            pltpu.VMEM((cols // 8, 8, 128), f32),
            pltpu.VMEM((2, children, sides, NX, OWNERS, 16, WIDTH), bf16),
            pltpu.VMEM((2, children, sides, NX - 1, OWNERS, 16, WIDTH), bf16),
            pltpu.VMEM((children, sides, NZ, 16, WIDTH), bf16),
            pltpu.VMEM((children, sides, NZ - 1, 16, WIDTH), bf16),
            pltpu.VMEM((cols // 128, 128), f32),
            pltpu.VMEM((NX - 1, cols // 128, 128), f32),
            pltpu.VMEM((cols // 128, 128), f32),
            pltpu.VMEM((NZ - 1, cols // 128, 128), f32),
            dma((6,)),
            dma((2, children, NX)),
            dma((2, children, sides, NX - 1)),
            dma((2, children, sides, NX - 1)),
            dma((children, sides, NZ - 1)),
            dma((children, sides, NZ - 1)),
            dma((NX - 1,)),
            dma((NX - 1,)),
            dma((NZ - 1,)),
            dma((NZ - 1,)),
        ],
        compiler_params=pltpu.CompilerParams(
            collective_id=0, has_side_effects=True, vmem_limit_bytes=24 * 2**20
        ),
        name="panel_product",
    )(
        *(
            pltpu.with_memory_space_constraint(value, pltpu.HBM)
            for value in (
                child_vectors.reshape(children, NZ, NX, 16, half),
                merge_position,
                pole_frac,
                weights,
                retained,
                root_index.reshape(1, cols),
                root_offset.reshape(1, cols),
            )
        )
    )


def solution(mesh):
    return jax.shard_map(
        local,
        mesh=mesh,
        in_specs=(
            P(None, "row", "col"),
            P(None, "col"),
            P(None, "col"),
            P(None, "col"),
            P(None, "col"),
            P(),
            P(),
        ),
        out_specs=P(None, ("row", "col"), None),
        check_vma=False,
    )
```

```python
import jax
import jax.numpy as jnp
from jax import lax
from jax.experimental import pallas as pl
from jax.experimental.pallas import tpu as pltpu
from jax.sharding import PartitionSpec as P

NX = 4
NZ = 8
MESH = pl.DeviceIdType.MESH
OWNERS = NZ // 2
WIDTH = 256


def kernel(
    vectors_hbm,
    position_hbm,
    fraction_hbm,
    weight_hbm,
    keep_hbm,
    root_hbm,
    offset_hbm,
    out_ref,
    position_ref,
    fraction_ref,
    weight_ref,
    keep_ref,
    root_ref,
    offset_ref,
    vectors,
    panel,
    poles,
    roots,
    squares,
    part,
    arrived,
    spread,
    landed,
    own_total,
    x_totals,
    z_own,
    z_totals,
    scale,
    x_ready,
    z_ready,
    small_sem,
    load_sem,
    x_send,
    x_recv,
    z_send,
    z_recv,
    tx_send,
    tx_recv,
    tz_send,
    tz_recv,
):
    small = []
    for n, (source, target) in enumerate(
        (
            (root_hbm, root_ref),
            (offset_hbm, offset_ref),
            (position_hbm, position_ref),
            (fraction_hbm, fraction_ref),
            (weight_hbm, weight_ref),
            (keep_hbm, keep_ref),
        )
    ):
        copy = pltpu.make_async_copy(source, target, small_sem.at[n])
        copy.start()
        small.append(copy)

    col = lax.axis_index("col")
    z = col // NX
    x = col % NX

    def at(zz, xx):
        return {"col": zz * NX + xx}

    x_peers = [(x + d) % NX for d in (2, 1, 3)]
    z_peers = [(z + d) % NZ for d in (4, 3, 5, 2, 6, 1, 7)]

    hub_x = 3 - (z // 6 - z // 7)
    hub_z = 7 - x // 3
    barrier = pltpu.get_barrier_semaphore()

    @pl.when(x != hub_x)
    def _():
        pl.semaphore_signal(barrier, inc=1, device_id=at(z, hub_x), device_id_type=MESH)

    @pl.when(z != hub_z)
    def _():
        pl.semaphore_signal(barrier, inc=1, device_id=at(hub_z, x), device_id_type=MESH)

    def answer():
        @pl.when(x == hub_x)
        def _():
            pl.semaphore_wait(barrier, NX - 1)
            for xx in x_peers:
                pl.semaphore_signal(x_ready, inc=1, device_id=at(z, xx), device_id_type=MESH)

        @pl.when(z == hub_z)
        def _():
            pl.semaphore_wait(barrier, NZ - 1)
            for zz in z_peers:
                pl.semaphore_signal(z_ready, inc=1, device_id=at(zz, x), device_id_type=MESH)

    def load(group, child, xx):
        return pltpu.make_async_copy(
            vectors_hbm.at[child, pl.ds(group * OWNERS, OWNERS), xx],
            vectors.at[group, child, xx],
            load_sem.at[group, child, xx],
        )

    def wait_loads(group, child):
        for xx in range(NX):
            load(group, child, xx).wait()

    def start_loads(group, child):
        for xx in range(NX):
            load(group, child, xx).start()

    start_loads(0, 0)
    for copy in small:
        copy.wait()

    half = position_ref.shape[1]
    for child in range(2):
        row = slice(child, child + 1)
        poles[child, 0] = jnp.broadcast_to(position_ref[row, :].astype(jnp.float32), (8, half))
        poles[child, 1] = jnp.broadcast_to(fraction_ref[row, :], (8, half))
        poles[child, 2] = jnp.broadcast_to(
            keep_ref[row, :].astype(jnp.float32) * weight_ref[row, :], (8, half)
        )
    for block in range(4):
        lanes = slice(block * 128, block * 128 + 128)
        roots[0, block * 16 : block * 16 + 16] = jnp.broadcast_to(
            root_ref[:, lanes].astype(jnp.float32), (128, 128)
        ).T.reshape(16, 8, 128)
        roots[1, block * 16 : block * 16 + 16] = jnp.broadcast_to(
            offset_ref[:, lanes], (128, 128)
        ).T.reshape(16, 8, 128)

    squares[...] = jnp.zeros_like(squares)

    def make_panel(child, side, start, stop):
        def body(step, carry):
            first = side * 32 + step * 4
            root_rows = roots[0, pl.ds(first, 4)]
            offset_rows = roots[1, pl.ds(first, 4)]
            total = jnp.zeros((4, 8, 128), jnp.float32)
            for block in range(half // 128):
                lanes = slice(block * 128, block * 128 + 128)
                spacing = (poles[child, 0, :, lanes][None] - root_rows) + (
                    poles[child, 1, :, lanes][None] - offset_rows
                )
                raw = poles[child, 2, :, lanes][None] / spacing
                total = total + raw * raw
                panel[child, pl.ds(pl.multiple_of(first * 8, 32), 32), lanes] = raw.reshape(
                    32, 128
                ).astype(jnp.bfloat16)
            squares[pl.ds(first, 4)] = squares[pl.ds(first, 4)] + total
            return carry

        lax.fori_loop(start, stop, body, 0)

    def remote(src, dst, send, recv, target):
        return pltpu.make_async_remote_copy(
            src_ref=src, dst_ref=dst, send_sem=send, recv_sem=recv, device_id=target, device_id_type=MESH
        )

    def product(group, child, columns):
        return lax.dot_general(
            vectors[group, child].reshape(NX * OWNERS * 16, half),
            panel[child, columns],
            (((1,), (1,)), ((), ())),
            preferred_element_type=jnp.float32,
        ).astype(jnp.bfloat16)

    def x_copy(group, child, side, n):
        return remote(
            part.at[group, child, side, x_peers[n]],
            arrived.at[group, child, side, n],
            x_send.at[group, child, side, n],
            x_recv.at[group, child, side, n],
            at(z, x_peers[n]),
        )

    def send_x(group, child, side):
        for n in range(NX - 1):
            x_copy(group, child, side, n).start()

    def z_copy(child, side, n):
        return remote(
            spread.at[child, side, z_peers[n]],
            landed.at[child, side, n],
            z_send.at[child, side, n],
            z_recv.at[child, side, n],
            at(z_peers[n], x),
        )

    def send_z(group, child, side):
        total = part[group, child, side, x].astype(jnp.float32)
        for n in range(NX - 1):
            x_copy(group, child, side, n).wait_recv()
            total = total + arrived[group, child, side, n].astype(jnp.float32)
        spread[child, side, pl.ds(group * OWNERS, OWNERS)] = total.astype(jnp.bfloat16)
        for n, zz in enumerate(z_peers):

            @pl.when(zz // OWNERS == group)
            def _(n=n):
                z_copy(child, side, n).start()

    def tx_copy(n):
        return remote(own_total, x_totals.at[n], tx_send.at[n], tx_recv.at[n], at(z, x_peers[n]))

    def tz_copy(n):
        return remote(z_own, z_totals.at[n], tz_send.at[n], tz_recv.at[n], at(z_peers[n], x))

    def loop(count):
        def run(body):
            lax.fori_loop(0, count, lambda step, carry: (body(step), carry)[1], 0)

        return run

    @loop(4)
    def _(unit):
        child, side = unit // 2, unit % 2
        make_panel(child, side, 0, 4)
        pl.when(unit == 0)(answer)
        make_panel(child, side, 4, 8)

        @pl.when(side == 0)
        def _():
            wait_loads(0, child)

        @pl.when(unit == 0)
        def _():
            start_loads(0, 1)
            start_loads(1, 0)
            start_loads(1, 1)

        columns = pl.ds(pl.multiple_of(side * WIDTH, WIDTH), WIDTH)
        part[0, child, side] = product(0, child, columns).reshape(NX, OWNERS, 16, WIDTH)

        @pl.when(jnp.logical_and(unit == 0, x != hub_x))
        def _():
            pl.semaphore_wait(x_ready, 1)

        @pl.when(unit == 3)
        def _():
            for block in range(4):
                own_total[block : block + 1] = jnp.sum(
                    squares[block * 16 : block * 16 + 16].reshape(128, 128).T, axis=0, keepdims=True
                )
            for n in range(NX - 1):
                tx_copy(n).start()

        send_x(0, child, side)

    @loop(2)
    def _(child):
        wait_loads(1, child)
        block = product(1, child, slice(None))
        for side in range(2):
            part[1, child, side] = block[:, side * WIDTH : side * WIDTH + WIDTH].reshape(NX, OWNERS, 16, WIDTH)
        for side in range(2):
            send_x(1, child, side)

        @pl.when(jnp.logical_and(child == 0, z != hub_z))
        def _():
            pl.semaphore_wait(z_ready, 1)

        send_z(0, 0, child)

    @loop(6)
    def _(step):
        unit = step + 2
        group, child, side = unit // 4, unit // 2 % 2, unit % 2

        @pl.when(step == 1)
        def _():
            for n in range(NX - 1):
                tx_copy(n).wait_recv()
            z_own[...] = own_total[...] + x_totals[0] + x_totals[1] + x_totals[2]
            for n in range(NZ - 1):
                tz_copy(n).start()

        send_z(group, child, side)

    total = z_own[...]
    for n in range(NZ - 1):
        tz_copy(n).wait_recv()
        total = total + z_totals[n]
    scale[...] = lax.rsqrt(total)

    @loop(4)
    def _(unit):
        child, side = unit // 2, unit % 2
        result = spread[child, side, z].astype(jnp.float32)
        for n in range(NZ - 1):
            z_copy(child, side, n).wait_recv()
            result = result + landed[child, side, n].astype(jnp.float32)
        for block in range(2):
            first = pl.multiple_of(side * WIDTH + block * 128, 128)
            out_ref[child, :, pl.ds(first, 128)] = (
                result[:, block * 128 : block * 128 + 128] * scale[pl.ds(side * 2 + block, 1)]
            ).astype(jnp.bfloat16)

    @loop(4)
    def _(unit):
        child, side = unit // 2, unit % 2
        for n in range(NX - 1):
            x_copy(0, child, side, n).wait_send()
            x_copy(1, child, side, n).wait_send()
        for n in range(NZ - 1):
            z_copy(child, side, n).wait_send()

    for n in range(NX - 1):
        tx_copy(n).wait_send()
    for n in range(NZ - 1):
        tz_copy(n).wait_send()


def local(child_vectors, merge_position, pole_frac, weights, retained, root_index, root_offset):
    children, rows, half = child_vectors.shape
    cols = root_index.shape[0]
    bf16, f32 = jnp.bfloat16, jnp.float32
    dma = pltpu.SemaphoreType.DMA
    sides = cols // WIDTH
    return pl.pallas_call(
        kernel,
        out_shape=jax.ShapeDtypeStruct((children, 16, cols), bf16),
        in_specs=[pl.BlockSpec(memory_space=pltpu.HBM)] * 7,
        out_specs=pl.BlockSpec(memory_space=pltpu.VMEM),
        scratch_shapes=[
            pltpu.VMEM((children, half), jnp.int32),
            pltpu.VMEM((children, half), f32),
            pltpu.VMEM((children, half), f32),
            pltpu.VMEM((children, half), jnp.int32),
            pltpu.VMEM((1, cols), jnp.int32),
            pltpu.VMEM((1, cols), f32),
            pltpu.VMEM((2, children, NX, OWNERS, 16, half), bf16),
            pltpu.VMEM((children, cols, half), bf16),
            pltpu.VMEM((children, 3, 8, half), f32),
            pltpu.VMEM((2, cols // 8, 8, 128), f32),
            pltpu.VMEM((cols // 8, 8, 128), f32),
            pltpu.VMEM((2, children, sides, NX, OWNERS, 16, WIDTH), bf16),
            pltpu.VMEM((2, children, sides, NX - 1, OWNERS, 16, WIDTH), bf16),
            pltpu.VMEM((children, sides, NZ, 16, WIDTH), bf16),
            pltpu.VMEM((children, sides, NZ - 1, 16, WIDTH), bf16),
            pltpu.VMEM((cols // 128, 128), f32),
            pltpu.VMEM((NX - 1, cols // 128, 128), f32),
            pltpu.VMEM((cols // 128, 128), f32),
            pltpu.VMEM((NZ - 1, cols // 128, 128), f32),
            pltpu.VMEM((cols // 128, 128), f32),
            pltpu.SemaphoreType.REGULAR,
            pltpu.SemaphoreType.REGULAR,
            dma((6,)),
            dma((2, children, NX)),
            dma((2, children, sides, NX - 1)),
            dma((2, children, sides, NX - 1)),
            dma((children, sides, NZ - 1)),
            dma((children, sides, NZ - 1)),
            dma((NX - 1,)),
            dma((NX - 1,)),
            dma((NZ - 1,)),
            dma((NZ - 1,)),
        ],
        compiler_params=pltpu.CompilerParams(
            collective_id=0, has_side_effects=True, vmem_limit_bytes=24 * 2**20
        ),
        name="panel_product",
    )(
        *(
            pltpu.with_memory_space_constraint(value, pltpu.HBM)
            for value in (
                child_vectors.reshape(children, NZ, NX, 16, half),
                merge_position,
                pole_frac,
                weights,
                retained,
                root_index.reshape(1, cols),
                root_offset.reshape(1, cols),
            )
        )
    )


def solution(mesh):
    return jax.shard_map(
        local,
        mesh=mesh,
        in_specs=(
            P(None, "row", "col"),
            P(None, "col"),
            P(None, "col"),
            P(None, "col"),
            P(None, "col"),
            P(),
            P(),
        ),
        out_specs=P(None, ("row", "col"), None),
        check_vma=False,
    )
```

```python
import jax
import jax.numpy as jnp
from jax import lax
from jax.experimental import pallas as pl
from jax.experimental.pallas import tpu as pltpu
from jax.sharding import PartitionSpec as P

NX = 4
NZ = 8
MESH = pl.DeviceIdType.MESH
OWNERS = NZ // 2
WIDTH = 256


def kernel(
    vectors_hbm,
    position_hbm,
    fraction_hbm,
    weight_hbm,
    keep_hbm,
    root_hbm,
    offset_hbm,
    out_ref,
    position_ref,
    fraction_ref,
    weight_ref,
    keep_ref,
    root_ref,
    offset_ref,
    vectors,
    panel,
    poles,
    roots,
    squares,
    part,
    arrived,
    spread,
    landed,
    own_total,
    x_totals,
    z_own,
    z_totals,
    scale,
    x_ready,
    z_ready,
    small_sem,
    load_sem,
    x_send,
    x_recv,
    z_send,
    z_recv,
    tx_send,
    tx_recv,
    tz_send,
    tz_recv,
):
    small = []
    for n, (source, target) in enumerate(
        (
            (root_hbm, root_ref),
            (offset_hbm, offset_ref),
            (position_hbm, position_ref),
            (fraction_hbm, fraction_ref),
            (weight_hbm, weight_ref),
            (keep_hbm, keep_ref),
        )
    ):
        copy = pltpu.make_async_copy(source, target, small_sem.at[n])
        copy.start()
        small.append(copy)

    col = lax.axis_index("col")
    z = col // NX
    x = col % NX

    def at(zz, xx):
        return {"col": zz * NX + xx}

    x_peers = [(x + d) % NX for d in (2, 1, 3)]
    z_peers = [(z + d) % NZ for d in (4, 3, 5, 2, 6, 1, 7)]

    hub_x = 3 - (z // 6 - z // 7)
    hub_z = 7 - x // 3
    barrier = pltpu.get_barrier_semaphore()

    @pl.when(x != hub_x)
    def _():
        pl.semaphore_signal(barrier, inc=1, device_id=at(z, hub_x), device_id_type=MESH)

    @pl.when(z != hub_z)
    def _():
        pl.semaphore_signal(barrier, inc=1, device_id=at(hub_z, x), device_id_type=MESH)

    def answer():
        @pl.when(x == hub_x)
        def _():
            pl.semaphore_wait(barrier, NX - 1)
            for xx in x_peers:
                pl.semaphore_signal(x_ready, inc=1, device_id=at(z, xx), device_id_type=MESH)

        @pl.when(z == hub_z)
        def _():
            pl.semaphore_wait(barrier, NZ - 1)
            for zz in z_peers:
                pl.semaphore_signal(z_ready, inc=1, device_id=at(zz, x), device_id_type=MESH)

    def load(group, child, xx):
        return pltpu.make_async_copy(
            vectors_hbm.at[child, pl.ds(group * OWNERS, OWNERS), xx],
            vectors.at[group, child, xx],
            load_sem.at[group, child],
        )

    def wait_all(ref, sem):
        pltpu.make_async_copy(ref, ref, sem).wait()

    def wait_loads(group, child):
        wait_all(vectors.at[group, child], load_sem.at[group, child])

    def start_loads(group, child):
        for xx in range(NX):
            load(group, child, xx).start()

    start_loads(0, 0)
    for copy in small:
        copy.wait()

    half = position_ref.shape[1]
    for child in range(2):
        row = slice(child, child + 1)
        poles[child, 0] = jnp.broadcast_to(position_ref[row, :].astype(jnp.float32), (8, half))
        poles[child, 1] = jnp.broadcast_to(fraction_ref[row, :], (8, half))
        poles[child, 2] = jnp.broadcast_to(
            keep_ref[row, :].astype(jnp.float32) * weight_ref[row, :], (8, half)
        )
    for block in range(4):
        lanes = slice(block * 128, block * 128 + 128)
        roots[0, block * 16 : block * 16 + 16] = jnp.broadcast_to(
            root_ref[:, lanes].astype(jnp.float32), (128, 128)
        ).T.reshape(16, 8, 128)
        roots[1, block * 16 : block * 16 + 16] = jnp.broadcast_to(
            offset_ref[:, lanes], (128, 128)
        ).T.reshape(16, 8, 128)

    squares[...] = jnp.zeros_like(squares)

    def make_panel(child, side, start, stop):
        def body(step, carry):
            first = side * 32 + step * 4
            root_rows = roots[0, pl.ds(first, 4)]
            offset_rows = roots[1, pl.ds(first, 4)]
            total = jnp.zeros((4, 8, 128), jnp.float32)
            for block in range(half // 128):
                lanes = slice(block * 128, block * 128 + 128)
                spacing = (poles[child, 0, :, lanes][None] - root_rows) + (
                    poles[child, 1, :, lanes][None] - offset_rows
                )
                raw = poles[child, 2, :, lanes][None] / spacing
                total = total + raw * raw
                panel[child, pl.ds(pl.multiple_of(first * 8, 32), 32), lanes] = raw.reshape(
                    32, 128
                ).astype(jnp.bfloat16)
            squares[pl.ds(first, 4)] = squares[pl.ds(first, 4)] + total
            return carry

        lax.fori_loop(start, stop, body, 0)

    def remote(src, dst, send, recv, target):
        return pltpu.make_async_remote_copy(
            src_ref=src, dst_ref=dst, send_sem=send, recv_sem=recv, device_id=target, device_id_type=MESH
        )

    def product(group, child, columns):
        return lax.dot_general(
            vectors[group, child].reshape(NX * OWNERS * 16, half),
            panel[child, columns],
            (((1,), (1,)), ((), ())),
            preferred_element_type=jnp.float32,
        ).astype(jnp.bfloat16)

    def x_copy(group, child, side, n):
        return remote(
            part.at[group, child, side, x_peers[n]],
            arrived.at[group, child, side, n],
            x_send,
            x_recv.at[group, child, side],
            at(z, x_peers[n]),
        )

    def send_x(group, child, side):
        for n in range(NX - 1):
            x_copy(group, child, side, n).start()

    def z_copy(child, side, n):
        return remote(
            spread.at[child, side, z_peers[n]],
            landed.at[child, side, n],
            z_send,
            z_recv.at[child, side],
            at(z_peers[n], x),
        )

    def send_z(group, child, side):
        total = part[group, child, side, x].astype(jnp.float32)
        wait_all(arrived.at[group, child, side], x_recv.at[group, child, side])
        for n in range(NX - 1):
            total = total + arrived[group, child, side, n].astype(jnp.float32)
        spread[child, side, pl.ds(group * OWNERS, OWNERS)] = total.astype(jnp.bfloat16)
        for n, zz in enumerate(z_peers):

            @pl.when(zz // OWNERS == group)
            def _(n=n):
                z_copy(child, side, n).start()

    def tx_copy(n):
        return remote(own_total, x_totals.at[n], tx_send, tx_recv, at(z, x_peers[n]))

    def tz_copy(n):
        return remote(z_own, z_totals.at[n], tz_send, tz_recv, at(z_peers[n], x))

    def loop(count):
        def run(body):
            lax.fori_loop(0, count, lambda step, carry: (body(step), carry)[1], 0)

        return run

    @loop(4)
    def _(unit):
        child, side = unit // 2, unit % 2
        make_panel(child, side, 0, 4)
        pl.when(unit == 0)(answer)
        make_panel(child, side, 4, 8)

        @pl.when(side == 0)
        def _():
            wait_loads(0, child)

        @pl.when(unit == 0)
        def _():
            start_loads(0, 1)
            start_loads(1, 0)
            start_loads(1, 1)

        columns = pl.ds(pl.multiple_of(side * WIDTH, WIDTH), WIDTH)
        part[0, child, side] = product(0, child, columns).reshape(NX, OWNERS, 16, WIDTH)

        @pl.when(jnp.logical_and(unit == 0, x != hub_x))
        def _():
            pl.semaphore_wait(x_ready, 1)

        @pl.when(unit == 3)
        def _():
            for block in range(4):
                own_total[block : block + 1] = jnp.sum(
                    squares[block * 16 : block * 16 + 16].reshape(128, 128).T, axis=0, keepdims=True
                )
            for n in range(NX - 1):
                tx_copy(n).start()

        send_x(0, child, side)

    @loop(2)
    def _(child):
        wait_loads(1, child)
        block = product(1, child, slice(None))
        for side in range(2):
            part[1, child, side] = block[:, side * WIDTH : side * WIDTH + WIDTH].reshape(NX, OWNERS, 16, WIDTH)
        for side in range(2):
            send_x(1, child, side)

        @pl.when(jnp.logical_and(child == 0, z != hub_z))
        def _():
            pl.semaphore_wait(z_ready, 1)

        send_z(0, 0, child)

    @loop(6)
    def _(step):
        unit = step + 2
        group, child, side = unit // 4, unit // 2 % 2, unit % 2

        @pl.when(step == 1)
        def _():
            wait_all(x_totals, tx_recv)
            z_own[...] = own_total[...] + x_totals[0] + x_totals[1] + x_totals[2]
            for n in range(NZ - 1):
                tz_copy(n).start()

        send_z(group, child, side)

    total = z_own[...]
    wait_all(z_totals, tz_recv)
    for n in range(NZ - 1):
        total = total + z_totals[n]
    scale[...] = lax.rsqrt(total)

    @loop(4)
    def _(unit):
        child, side = unit // 2, unit % 2
        result = spread[child, side, z].astype(jnp.float32)
        wait_all(landed.at[child, side], z_recv.at[child, side])
        for n in range(NZ - 1):
            result = result + landed[child, side, n].astype(jnp.float32)
        for block in range(2):
            first = pl.multiple_of(side * WIDTH + block * 128, 128)
            out_ref[child, :, pl.ds(first, 128)] = (
                result[:, block * 128 : block * 128 + 128] * scale[pl.ds(side * 2 + block, 1)]
            ).astype(jnp.bfloat16)

    wait_all(arrived, x_send)
    wait_all(landed, z_send)
    wait_all(x_totals, tx_send)
    wait_all(z_totals, tz_send)


def local(child_vectors, merge_position, pole_frac, weights, retained, root_index, root_offset):
    children, rows, half = child_vectors.shape
    cols = root_index.shape[0]
    bf16, f32 = jnp.bfloat16, jnp.float32
    dma = pltpu.SemaphoreType.DMA
    sides = cols // WIDTH
    return pl.pallas_call(
        kernel,
        out_shape=jax.ShapeDtypeStruct((children, 16, cols), bf16),
        in_specs=[pl.BlockSpec(memory_space=pltpu.HBM)] * 7,
        out_specs=pl.BlockSpec(memory_space=pltpu.VMEM),
        scratch_shapes=[
            pltpu.VMEM((children, half), jnp.int32),
            pltpu.VMEM((children, half), f32),
            pltpu.VMEM((children, half), f32),
            pltpu.VMEM((children, half), jnp.int32),
            pltpu.VMEM((1, cols), jnp.int32),
            pltpu.VMEM((1, cols), f32),
            pltpu.VMEM((2, children, NX, OWNERS, 16, half), bf16),
            pltpu.VMEM((children, cols, half), bf16),
            pltpu.VMEM((children, 3, 8, half), f32),
            pltpu.VMEM((2, cols // 8, 8, 128), f32),
            pltpu.VMEM((cols // 8, 8, 128), f32),
            pltpu.VMEM((2, children, sides, NX, OWNERS, 16, WIDTH), bf16),
            pltpu.VMEM((2, children, sides, NX - 1, OWNERS, 16, WIDTH), bf16),
            pltpu.VMEM((children, sides, NZ, 16, WIDTH), bf16),
            pltpu.VMEM((children, sides, NZ - 1, 16, WIDTH), bf16),
            pltpu.VMEM((cols // 128, 128), f32),
            pltpu.VMEM((NX - 1, cols // 128, 128), f32),
            pltpu.VMEM((cols // 128, 128), f32),
            pltpu.VMEM((NZ - 1, cols // 128, 128), f32),
            pltpu.VMEM((cols // 128, 128), f32),
            pltpu.SemaphoreType.REGULAR,
            pltpu.SemaphoreType.REGULAR,
            dma((6,)),
            dma((2, children)),
            dma,
            dma((2, children, sides)),
            dma,
            dma((children, sides)),
            dma,
            dma,
            dma,
            dma,
        ],
        compiler_params=pltpu.CompilerParams(
            collective_id=0, has_side_effects=True, vmem_limit_bytes=24 * 2**20
        ),
        name="panel_product",
    )(
        *(
            pltpu.with_memory_space_constraint(value, pltpu.HBM)
            for value in (
                child_vectors.reshape(children, NZ, NX, 16, half),
                merge_position,
                pole_frac,
                weights,
                retained,
                root_index.reshape(1, cols),
                root_offset.reshape(1, cols),
            )
        )
    )


def solution(mesh):
    return jax.shard_map(
        local,
        mesh=mesh,
        in_specs=(
            P(None, "row", "col"),
            P(None, "col"),
            P(None, "col"),
            P(None, "col"),
            P(None, "col"),
            P(),
            P(),
        ),
        out_specs=P(None, ("row", "col"), None),
        check_vma=False,
    )
```

```python
import jax
import jax.numpy as jnp
from jax import lax
from jax.experimental import pallas as pl
from jax.experimental.pallas import tpu as pltpu
from jax.sharding import PartitionSpec as P

NX = 4
NZ = 8
MESH = pl.DeviceIdType.MESH
OWNERS = NZ // 2
WIDTH = 256


def kernel(
    vectors_hbm,
    position_hbm,
    fraction_hbm,
    weight_hbm,
    keep_hbm,
    root_hbm,
    offset_hbm,
    out_ref,
    position_ref,
    fraction_ref,
    weight_ref,
    keep_ref,
    root_ref,
    offset_ref,
    vectors,
    panel,
    poles,
    roots,
    squares,
    part,
    arrived,
    spread,
    landed,
    own_total,
    x_totals,
    z_own,
    z_totals,
    scale,
    x_ready,
    z_ready,
    small_sem,
    load_sem,
    x_send,
    x_recv,
    z_send,
    z_recv,
    tx_send,
    tx_recv,
    tz_send,
    tz_recv,
):
    small = []
    for n, (source, target) in enumerate(
        (
            (root_hbm, root_ref),
            (offset_hbm, offset_ref),
            (position_hbm, position_ref),
            (fraction_hbm, fraction_ref),
            (weight_hbm, weight_ref),
            (keep_hbm, keep_ref),
        )
    ):
        copy = pltpu.make_async_copy(source, target, small_sem.at[n])
        copy.start()
        small.append(copy)

    col = lax.axis_index("col")
    z = lax.div(col, NX)
    x = lax.rem(col, NX)

    def at(zz, xx):
        return {"col": zz * NX + xx}

    x_peers = [lax.rem(x + d, NX) for d in (2, 1, 3)]
    z_peers = [lax.rem(z + d, NZ) for d in (4, 3, 5, 2, 6, 1, 7)]

    hub_x = 3 - (lax.div(z, 6) - lax.div(z, 7))
    hub_z = 7 - lax.div(x, 3)
    half_z = lax.div(z, OWNERS)
    barrier = pltpu.get_barrier_semaphore()

    @pl.when(x != hub_x)
    def _():
        pl.semaphore_signal(barrier, inc=1, device_id=at(z, hub_x), device_id_type=MESH)

    @pl.when(z != hub_z)
    def _():
        pl.semaphore_signal(barrier, inc=1, device_id=at(hub_z, x), device_id_type=MESH)

    def answer():
        @pl.when(x == hub_x)
        def _():
            pl.semaphore_wait(barrier, NX - 1)
            for xx in x_peers:
                pl.semaphore_signal(x_ready, inc=1, device_id=at(z, xx), device_id_type=MESH)

        @pl.when(z == hub_z)
        def _():
            pl.semaphore_wait(barrier, NZ - 1)
            for zz in z_peers:
                pl.semaphore_signal(z_ready, inc=1, device_id=at(zz, x), device_id_type=MESH)

    def load(group, child, xx):
        return pltpu.make_async_copy(
            vectors_hbm.at[child, pl.ds(group * OWNERS, OWNERS), xx],
            vectors.at[group, child, xx],
            load_sem.at[group, child],
        )

    def wait_all(ref, sem):
        pltpu.make_async_copy(ref, ref, sem).wait()

    def wait_loads(group, child):
        wait_all(vectors.at[group, child], load_sem.at[group, child])

    def start_loads(group, child):
        for xx in range(NX):
            load(group, child, xx).start()

    start_loads(0, 0)
    for copy in small:
        copy.wait()

    half = position_ref.shape[1]
    for child in range(2):
        row = slice(child, child + 1)
        poles[child, 0] = jnp.broadcast_to(position_ref[row, :].astype(jnp.float32), (8, half))
        poles[child, 1] = jnp.broadcast_to(fraction_ref[row, :], (8, half))
        poles[child, 2] = jnp.broadcast_to(
            keep_ref[row, :].astype(jnp.float32) * weight_ref[row, :], (8, half)
        )
    for block in range(4):
        lanes = slice(block * 128, block * 128 + 128)
        roots[0, block * 16 : block * 16 + 16] = jnp.broadcast_to(
            root_ref[:, lanes].astype(jnp.float32), (128, 128)
        ).T.reshape(16, 8, 128)
        roots[1, block * 16 : block * 16 + 16] = jnp.broadcast_to(
            offset_ref[:, lanes], (128, 128)
        ).T.reshape(16, 8, 128)

    squares[...] = jnp.zeros_like(squares)

    def make_panel(child, side, start, stop):
        def body(step, carry):
            first = side * 32 + step * 4
            root_rows = roots[0, pl.ds(first, 4)]
            offset_rows = roots[1, pl.ds(first, 4)]
            total = jnp.zeros((4, 8, 128), jnp.float32)
            for block in range(half // 128):
                lanes = slice(block * 128, block * 128 + 128)
                spacing = (poles[child, 0, :, lanes][None] - root_rows) + (
                    poles[child, 1, :, lanes][None] - offset_rows
                )
                raw = poles[child, 2, :, lanes][None] / spacing
                total = total + raw * raw
                panel[child, pl.ds(pl.multiple_of(first * 8, 32), 32), lanes] = raw.reshape(
                    32, 128
                ).astype(jnp.bfloat16)
            squares[pl.ds(first, 4)] = squares[pl.ds(first, 4)] + total
            return carry

        lax.fori_loop(start, stop, body, 0)

    def remote(src, dst, send, recv, target):
        return pltpu.make_async_remote_copy(
            src_ref=src, dst_ref=dst, send_sem=send, recv_sem=recv, device_id=target, device_id_type=MESH
        )

    def product(group, child, columns):
        return lax.dot_general(
            vectors[group, child].reshape(NX * OWNERS * 16, half),
            panel[child, columns],
            (((1,), (1,)), ((), ())),
            preferred_element_type=jnp.float32,
        ).astype(jnp.bfloat16)

    def x_copy(group, child, side, n):
        return remote(
            part.at[group, child, side, x_peers[n]],
            arrived.at[group, child, side, n],
            x_send,
            x_recv.at[group, child, side],
            at(z, x_peers[n]),
        )

    def send_x(group, child, side):
        for n in range(NX - 1):
            x_copy(group, child, side, n).start()

    def send_z(group, child, side, total):
        owners = pl.ds(group * OWNERS, OWNERS)
        spread[child, side, owners] = total.astype(jnp.bfloat16)
        for n in range(OWNERS):
            zz = group * OWNERS + n

            @pl.when(zz != z)
            def _(zz=zz):
                remote(
                    spread.at[child, side, zz],
                    landed.at[child, side, z],
                    z_send,
                    z_recv.at[child, side],
                    at(zz, x),
                ).start()

        @pl.when(half_z == group)
        def _():
            landed[child, side, z] = spread[child, side, z]

    def gather(group, child, side):
        total = part[group, child, side, x].astype(jnp.float32)
        wait_all(arrived.at[group, child, side], x_recv.at[group, child, side])
        for n in range(NX - 1):
            total = total + arrived[group, child, side, n].astype(jnp.float32)
        send_z(group, child, side, total)

    def tx_copy(n):
        return remote(own_total, x_totals.at[n], tx_send, tx_recv, at(z, x_peers[n]))

    def tz_copy(n):
        return remote(z_own, z_totals.at[n], tz_send, tz_recv, at(z_peers[n], x))

    def loop(count):
        def run(body):
            lax.fori_loop(0, count, lambda step, carry: (body(step), carry)[1], 0)

        return run

    @loop(4)
    def _(unit):
        child, side = unit // 2, unit % 2
        make_panel(child, side, 0, 4)
        pl.when(unit == 0)(answer)
        make_panel(child, side, 4, 8)

        @pl.when(side == 0)
        def _():
            wait_loads(0, child)

        @pl.when(unit == 0)
        def _():
            start_loads(0, 1)
            start_loads(1, 0)
            start_loads(1, 1)

        columns = pl.ds(pl.multiple_of(side * WIDTH, WIDTH), WIDTH)
        part[0, child, side] = product(0, child, columns).reshape(NX, OWNERS, 16, WIDTH)

        @pl.when(jnp.logical_and(unit == 0, x != hub_x))
        def _():
            pl.semaphore_wait(x_ready, 1)

        @pl.when(unit == 3)
        def _():
            for block in range(4):
                own_total[block : block + 1] = jnp.sum(
                    squares[block * 16 : block * 16 + 16].reshape(128, 128).T, axis=0, keepdims=True
                )
            for n in range(NX - 1):
                tx_copy(n).start()

        send_x(0, child, side)

    @loop(2)
    def _(child):
        wait_loads(1, child)
        block = product(1, child, slice(None))
        for side in range(2):
            part[1, child, side] = block[:, side * WIDTH : side * WIDTH + WIDTH].reshape(NX, OWNERS, 16, WIDTH)
        for side in range(2):
            send_x(1, child, side)

        @pl.when(jnp.logical_and(child == 0, z != hub_z))
        def _():
            pl.semaphore_wait(z_ready, 1)

        gather(0, 0, child)

    @loop(6)
    def _(step):
        unit = step + 2
        group, child, side = unit // 4, unit // 2 % 2, unit % 2

        @pl.when(step == 1)
        def _():
            wait_all(x_totals, tx_recv)
            z_own[...] = own_total[...] + x_totals[0] + x_totals[1] + x_totals[2]
            for n in range(NZ - 1):
                tz_copy(n).start()

        gather(group, child, side)

    total = z_own[...]
    wait_all(z_totals, tz_recv)
    for n in range(NZ - 1):
        total = total + z_totals[n]
    scale[...] = lax.rsqrt(total)

    @loop(4)
    def _(unit):
        child, side = unit // 2, unit % 2
        wait_all(landed.at[child, side, pl.ds(0, NZ - 1)], z_recv.at[child, side])
        result = landed[child, side, 0].astype(jnp.float32)
        for n in range(1, NZ):
            result = result + landed[child, side, n].astype(jnp.float32)
        for block in range(2):
            first = pl.multiple_of(side * WIDTH + block * 128, 128)
            out_ref[child, :, pl.ds(first, 128)] = (
                result[:, block * 128 : block * 128 + 128] * scale[pl.ds(side * 2 + block, 1)]
            ).astype(jnp.bfloat16)

    wait_all(arrived, x_send)
    wait_all(landed.at[:, :, pl.ds(0, NZ - 1)], z_send)
    wait_all(x_totals, tx_send)
    wait_all(z_totals, tz_send)


def local(child_vectors, merge_position, pole_frac, weights, retained, root_index, root_offset):
    children, rows, half = child_vectors.shape
    cols = root_index.shape[0]
    bf16, f32 = jnp.bfloat16, jnp.float32
    dma = pltpu.SemaphoreType.DMA
    sides = cols // WIDTH
    return pl.pallas_call(
        kernel,
        out_shape=jax.ShapeDtypeStruct((children, 16, cols), bf16),
        in_specs=[pl.BlockSpec(memory_space=pltpu.HBM)] * 7,
        out_specs=pl.BlockSpec(memory_space=pltpu.VMEM),
        scratch_shapes=[
            pltpu.VMEM((children, half), jnp.int32),
            pltpu.VMEM((children, half), f32),
            pltpu.VMEM((children, half), f32),
            pltpu.VMEM((children, half), jnp.int32),
            pltpu.VMEM((1, cols), jnp.int32),
            pltpu.VMEM((1, cols), f32),
            pltpu.VMEM((2, children, NX, OWNERS, 16, half), bf16),
            pltpu.VMEM((children, cols, half), bf16),
            pltpu.VMEM((children, 3, 8, half), f32),
            pltpu.VMEM((2, cols // 8, 8, 128), f32),
            pltpu.VMEM((cols // 8, 8, 128), f32),
            pltpu.VMEM((2, children, sides, NX, OWNERS, 16, WIDTH), bf16),
            pltpu.VMEM((2, children, sides, NX - 1, OWNERS, 16, WIDTH), bf16),
            pltpu.VMEM((children, sides, NZ, 16, WIDTH), bf16),
            pltpu.VMEM((children, sides, NZ, 16, WIDTH), bf16),
            pltpu.VMEM((cols // 128, 128), f32),
            pltpu.VMEM((NX - 1, cols // 128, 128), f32),
            pltpu.VMEM((cols // 128, 128), f32),
            pltpu.VMEM((NZ - 1, cols // 128, 128), f32),
            pltpu.VMEM((cols // 128, 128), f32),
            pltpu.SemaphoreType.REGULAR,
            pltpu.SemaphoreType.REGULAR,
            dma((6,)),
            dma((2, children)),
            dma,
            dma((2, children, sides)),
            dma,
            dma((children, sides)),
            dma,
            dma,
            dma,
            dma,
        ],
        compiler_params=pltpu.CompilerParams(
            collective_id=0, has_side_effects=True, vmem_limit_bytes=24 * 2**20
        ),
        name="panel_product",
    )(
        *(
            pltpu.with_memory_space_constraint(value, pltpu.HBM)
            for value in (
                child_vectors.reshape(children, NZ, NX, 16, half),
                merge_position,
                pole_frac,
                weights,
                retained,
                root_index.reshape(1, cols),
                root_offset.reshape(1, cols),
            )
        )
    )


def solution(mesh):
    return jax.shard_map(
        local,
        mesh=mesh,
        in_specs=(
            P(None, "row", "col"),
            P(None, "col"),
            P(None, "col"),
            P(None, "col"),
            P(None, "col"),
            P(),
            P(),
        ),
        out_specs=P(None, ("row", "col"), None),
        check_vma=False,
    )
```

```python
import jax
import jax.numpy as jnp
from jax import lax
from jax.experimental import pallas as pl
from jax.experimental.pallas import tpu as pltpu
from jax.sharding import PartitionSpec as P

NX = 4
NZ = 8
MESH = pl.DeviceIdType.MESH
OWNERS = NZ // 2
WIDTH = 256


def kernel(
    vectors_hbm,
    position_hbm,
    fraction_hbm,
    weight_hbm,
    keep_hbm,
    root_hbm,
    offset_hbm,
    out_ref,
    position_ref,
    fraction_ref,
    weight_ref,
    keep_ref,
    root_ref,
    offset_ref,
    vectors,
    panel,
    poles,
    roots,
    squares,
    part,
    arrived,
    spread,
    landed,
    own_total,
    x_totals,
    z_own,
    z_totals,
    scale,
    x_ready,
    z_ready,
    small_sem,
    load_sem,
    x_send,
    x_recv,
    z_send,
    z_recv,
    tx_send,
    tx_recv,
    tz_send,
    tz_recv,
):
    small = []
    for n, (source, target) in enumerate(
        (
            (root_hbm, root_ref),
            (offset_hbm, offset_ref),
            (position_hbm, position_ref),
            (fraction_hbm, fraction_ref),
            (weight_hbm, weight_ref),
            (keep_hbm, keep_ref),
        )
    ):
        copy = pltpu.make_async_copy(source, target, small_sem.at[n])
        copy.start()
        small.append(copy)

    col = lax.axis_index("col")
    z = lax.div(col, NX)
    x = lax.rem(col, NX)

    def at(zz, xx):
        return {"col": zz * NX + xx}

    x_peers = [lax.rem(x + d, NX) for d in (2, 1, 3)]
    z_peers = [lax.rem(z + d, NZ) for d in (4, 3, 5, 2, 6, 1, 7)]

    hub_x = 3 - (lax.div(z, 6) - lax.div(z, 7))
    hub_z = 7 - lax.div(x, 3)
    half_z = lax.div(z, OWNERS)
    barrier = pltpu.get_barrier_semaphore()

    @pl.when(x != hub_x)
    def _():
        pl.semaphore_signal(barrier, inc=1, device_id=at(z, hub_x), device_id_type=MESH)

    @pl.when(z != hub_z)
    def _():
        pl.semaphore_signal(barrier, inc=1, device_id=at(hub_z, x), device_id_type=MESH)

    def answer():
        @pl.when(x == hub_x)
        def _():
            pl.semaphore_wait(barrier, NX - 1)
            for xx in x_peers:
                pl.semaphore_signal(x_ready, inc=1, device_id=at(z, xx), device_id_type=MESH)

        @pl.when(z == hub_z)
        def _():
            pl.semaphore_wait(barrier, NZ - 1)
            for zz in z_peers:
                pl.semaphore_signal(z_ready, inc=1, device_id=at(zz, x), device_id_type=MESH)

    def load(group, child, xx):
        return pltpu.make_async_copy(
            vectors_hbm.at[child, pl.ds(group * OWNERS, OWNERS), xx],
            vectors.at[group, child, xx],
            load_sem.at[group, child],
        )

    def wait_all(ref, sem):
        pltpu.make_async_copy(ref, ref, sem).wait()

    def wait_loads(group, child):
        wait_all(vectors.at[group, child], load_sem.at[group, child])

    def start_loads(group, child):
        for xx in range(NX):
            load(group, child, xx).start()

    start_loads(0, 0)
    for copy in small:
        copy.wait()

    half = position_ref.shape[1]
    for child in range(2):
        row = slice(child, child + 1)
        poles[child, 0] = jnp.broadcast_to(position_ref[row, :].astype(jnp.float32), (8, half))
        poles[child, 1] = jnp.broadcast_to(fraction_ref[row, :], (8, half))
        poles[child, 2] = jnp.broadcast_to(
            keep_ref[row, :].astype(jnp.float32) * weight_ref[row, :], (8, half)
        )
    for block in range(4):
        lanes = slice(block * 128, block * 128 + 128)
        roots[0, block * 16 : block * 16 + 16] = jnp.broadcast_to(
            root_ref[:, lanes].astype(jnp.float32), (128, 128)
        ).T.reshape(16, 8, 128)
        roots[1, block * 16 : block * 16 + 16] = jnp.broadcast_to(
            offset_ref[:, lanes], (128, 128)
        ).T.reshape(16, 8, 128)

    squares[...] = jnp.zeros_like(squares)

    def make_panel(child, side, start, stop):
        def body(step, carry):
            first = side * 32 + step * 4
            root_rows = roots[0, pl.ds(first, 4)]
            offset_rows = roots[1, pl.ds(first, 4)]
            total = jnp.zeros((4, 8, 128), jnp.float32)
            for block in range(half // 128):
                lanes = slice(block * 128, block * 128 + 128)
                spacing = (poles[child, 0, :, lanes][None] - root_rows) + (
                    poles[child, 1, :, lanes][None] - offset_rows
                )
                raw = poles[child, 2, :, lanes][None] / spacing
                total = total + raw * raw
                panel[child, pl.ds(pl.multiple_of(first * 8, 32), 32), lanes] = raw.reshape(
                    32, 128
                ).astype(jnp.bfloat16)
            squares[pl.ds(first, 4)] = squares[pl.ds(first, 4)] + total
            return carry

        lax.fori_loop(start, stop, body, 0)

    def remote(src, dst, send, recv, target):
        return pltpu.make_async_remote_copy(
            src_ref=src, dst_ref=dst, send_sem=send, recv_sem=recv, device_id=target, device_id_type=MESH
        )

    def product(group, child, columns):
        return lax.dot_general(
            vectors[group, child].reshape(NX * OWNERS * 16, half),
            panel[child, columns],
            (((1,), (1,)), ((), ())),
            preferred_element_type=jnp.float32,
        ).astype(jnp.bfloat16)

    def x_copy(group, child, side, n):
        return remote(
            part.at[group, child, side, x_peers[n]],
            arrived.at[group, child, side, n],
            x_send,
            x_recv.at[group, child, side],
            at(z, x_peers[n]),
        )

    def send_x(group, child, side):
        for n in range(NX - 1):
            x_copy(group, child, side, n).start()

    def send_z(group, child, side, total):
        owners = pl.ds(group * OWNERS, OWNERS)
        spread[child, side, owners] = total.astype(jnp.bfloat16)
        for n in range(OWNERS):
            zz = group * OWNERS + n

            @pl.when(zz != z)
            def _(zz=zz):
                remote(
                    spread.at[child, side, zz],
                    landed.at[child, side, z],
                    z_send,
                    z_recv.at[child, side],
                    at(zz, x),
                ).start()

        @pl.when(half_z == group)
        def _():
            landed[child, side, z] = spread[child, side, z]

    def gather(group, child, side):
        total = part[group, child, side, x].astype(jnp.float32)
        wait_all(arrived.at[group, child, side], x_recv.at[group, child, side])
        for n in range(NX - 1):
            total = total + arrived[group, child, side, n].astype(jnp.float32)
        send_z(group, child, side, total)

    def tx_copy(n):
        return remote(own_total, x_totals.at[n], tx_send, tx_recv, at(z, x_peers[n]))

    def tz_copy(n):
        return remote(z_own, z_totals.at[n], tz_send, tz_recv, at(z_peers[n], x))

    def loop(count):
        def run(body):
            lax.fori_loop(0, count, lambda step, carry: (body(step), carry)[1], 0)

        return run

    @loop(4)
    def _(unit):
        child, side = unit // 2, unit % 2
        make_panel(child, side, 0, 4)
        pl.when(unit == 0)(answer)
        make_panel(child, side, 4, 8)

        @pl.when(side == 0)
        def _():
            wait_loads(0, child)

        @pl.when(unit == 0)
        def _():
            start_loads(0, 1)
            start_loads(1, 0)
            start_loads(1, 1)

        columns = pl.ds(pl.multiple_of(side * WIDTH, WIDTH), WIDTH)
        part[0, child, side] = product(0, child, columns).reshape(NX, OWNERS, 16, WIDTH)

        @pl.when(jnp.logical_and(unit == 0, x != hub_x))
        def _():
            pl.semaphore_wait(x_ready, 1)

        @pl.when(unit == 3)
        def _():
            for block in range(4):
                own_total[block : block + 1] = jnp.sum(
                    squares[block * 16 : block * 16 + 16].reshape(128, 128).T, axis=0, keepdims=True
                )
            for n in range(NX - 1):
                tx_copy(n).start()

        send_x(0, child, side)

    @pl.when(z != hub_z)
    def _():
        pl.semaphore_wait(z_ready, 1)

    gather(0, 0, 0)

    @loop(2)
    def _(child):
        wait_loads(1, child)
        block = product(1, child, slice(None))
        for side in range(2):
            part[1, child, side] = block[:, side * WIDTH : side * WIDTH + WIDTH].reshape(NX, OWNERS, 16, WIDTH)
        for side in range(2):
            send_x(1, child, side)


        @pl.when(child == 0)
        def _():
            gather(0, 0, 1)

    @loop(6)
    def _(step):
        unit = step + 2
        group, child, side = unit // 4, unit // 2 % 2, unit % 2

        @pl.when(step == 1)
        def _():
            wait_all(x_totals, tx_recv)
            z_own[...] = own_total[...] + x_totals[0] + x_totals[1] + x_totals[2]
            for n in range(NZ - 1):
                tz_copy(n).start()

        gather(group, child, side)

    total = z_own[...]
    wait_all(z_totals, tz_recv)
    for n in range(NZ - 1):
        total = total + z_totals[n]
    scale[...] = lax.rsqrt(total)

    @loop(4)
    def _(unit):
        child, side = unit // 2, unit % 2
        wait_all(landed.at[child, side, pl.ds(0, NZ - 1)], z_recv.at[child, side])
        result = landed[child, side, 0].astype(jnp.float32)
        for n in range(1, NZ):
            result = result + landed[child, side, n].astype(jnp.float32)
        for block in range(2):
            first = pl.multiple_of(side * WIDTH + block * 128, 128)
            out_ref[child, :, pl.ds(first, 128)] = (
                result[:, block * 128 : block * 128 + 128] * scale[pl.ds(side * 2 + block, 1)]
            ).astype(jnp.bfloat16)

    wait_all(arrived, x_send)
    wait_all(landed.at[:, :, pl.ds(0, NZ - 1)], z_send)
    wait_all(x_totals, tx_send)
    wait_all(z_totals, tz_send)


def local(child_vectors, merge_position, pole_frac, weights, retained, root_index, root_offset):
    children, rows, half = child_vectors.shape
    cols = root_index.shape[0]
    bf16, f32 = jnp.bfloat16, jnp.float32
    dma = pltpu.SemaphoreType.DMA
    sides = cols // WIDTH
    return pl.pallas_call(
        kernel,
        out_shape=jax.ShapeDtypeStruct((children, 16, cols), bf16),
        in_specs=[pl.BlockSpec(memory_space=pltpu.HBM)] * 7,
        out_specs=pl.BlockSpec(memory_space=pltpu.VMEM),
        scratch_shapes=[
            pltpu.VMEM((children, half), jnp.int32),
            pltpu.VMEM((children, half), f32),
            pltpu.VMEM((children, half), f32),
            pltpu.VMEM((children, half), jnp.int32),
            pltpu.VMEM((1, cols), jnp.int32),
            pltpu.VMEM((1, cols), f32),
            pltpu.VMEM((2, children, NX, OWNERS, 16, half), bf16),
            pltpu.VMEM((children, cols, half), bf16),
            pltpu.VMEM((children, 3, 8, half), f32),
            pltpu.VMEM((2, cols // 8, 8, 128), f32),
            pltpu.VMEM((cols // 8, 8, 128), f32),
            pltpu.VMEM((2, children, sides, NX, OWNERS, 16, WIDTH), bf16),
            pltpu.VMEM((2, children, sides, NX - 1, OWNERS, 16, WIDTH), bf16),
            pltpu.VMEM((children, sides, NZ, 16, WIDTH), bf16),
            pltpu.VMEM((children, sides, NZ, 16, WIDTH), bf16),
            pltpu.VMEM((cols // 128, 128), f32),
            pltpu.VMEM((NX - 1, cols // 128, 128), f32),
            pltpu.VMEM((cols // 128, 128), f32),
            pltpu.VMEM((NZ - 1, cols // 128, 128), f32),
            pltpu.VMEM((cols // 128, 128), f32),
            pltpu.SemaphoreType.REGULAR,
            pltpu.SemaphoreType.REGULAR,
            dma((6,)),
            dma((2, children)),
            dma,
            dma((2, children, sides)),
            dma,
            dma((children, sides)),
            dma,
            dma,
            dma,
            dma,
        ],
        compiler_params=pltpu.CompilerParams(
            collective_id=0, has_side_effects=True, vmem_limit_bytes=24 * 2**20
        ),
        name="panel_product",
    )(
        *(
            pltpu.with_memory_space_constraint(value, pltpu.HBM)
            for value in (
                child_vectors.reshape(children, NZ, NX, 16, half),
                merge_position,
                pole_frac,
                weights,
                retained,
                root_index.reshape(1, cols),
                root_offset.reshape(1, cols),
            )
        )
    )


def solution(mesh):
    return jax.shard_map(
        local,
        mesh=mesh,
        in_specs=(
            P(None, "row", "col"),
            P(None, "col"),
            P(None, "col"),
            P(None, "col"),
            P(None, "col"),
            P(),
            P(),
        ),
        out_specs=P(None, ("row", "col"), None),
        check_vma=False,
    )
```

```python
import jax
import jax.numpy as jnp
from jax import lax
from jax.experimental import pallas as pl
from jax.experimental.pallas import tpu as pltpu
from jax.sharding import PartitionSpec as P

NX = 4
NZ = 8
MESH = pl.DeviceIdType.MESH
OWNERS = NZ // 2
WIDTH = 256


def kernel(
    vectors_hbm,
    position_hbm,
    fraction_hbm,
    weight_hbm,
    keep_hbm,
    root_hbm,
    offset_hbm,
    out_ref,
    position_ref,
    fraction_ref,
    weight_ref,
    keep_ref,
    root_ref,
    offset_ref,
    vectors,
    panel,
    poles,
    roots,
    squares,
    part,
    arrived,
    ring,
    sent,
    spread,
    landed,
    own_total,
    x_totals,
    z_own,
    z_totals,
    scale,
    x_ready,
    z_ready,
    small_sem,
    load_sem,
    x_send,
    x_recv,
    r_send,
    r_recv,
    z_send,
    z_recv,
    tx_send,
    tx_recv,
    tz_send,
    tz_recv,
):
    small = []
    for n, (source, target) in enumerate(
        (
            (root_hbm, root_ref),
            (offset_hbm, offset_ref),
            (position_hbm, position_ref),
            (fraction_hbm, fraction_ref),
            (weight_hbm, weight_ref),
            (keep_hbm, keep_ref),
        )
    ):
        copy = pltpu.make_async_copy(source, target, small_sem.at[n])
        copy.start()
        small.append(copy)

    col = lax.axis_index("col")
    z = lax.div(col, NX)
    x = lax.rem(col, NX)

    def at(zz, xx):
        return {"col": zz * NX + xx}

    x_peers = [lax.rem(x + d, NX) for d in (2, 1, 3)]
    z_peers = [lax.rem(z + d, NZ) for d in (4, 3, 5, 2, 6, 1, 7)]

    hub_x = 3 - (lax.div(z, 6) - lax.div(z, 7))
    hub_z = 7 - lax.div(x, 3)
    half_z = lax.div(z, OWNERS)
    barrier = pltpu.get_barrier_semaphore()

    @pl.when(x != hub_x)
    def _():
        pl.semaphore_signal(barrier, inc=1, device_id=at(z, hub_x), device_id_type=MESH)

    @pl.when(z != hub_z)
    def _():
        pl.semaphore_signal(barrier, inc=1, device_id=at(hub_z, x), device_id_type=MESH)

    def answer():
        @pl.when(x == hub_x)
        def _():
            pl.semaphore_wait(barrier, NX - 1)
            for xx in x_peers:
                pl.semaphore_signal(x_ready, inc=1, device_id=at(z, xx), device_id_type=MESH)

        @pl.when(z == hub_z)
        def _():
            pl.semaphore_wait(barrier, NZ - 1)
            for zz in z_peers:
                pl.semaphore_signal(z_ready, inc=1, device_id=at(zz, x), device_id_type=MESH)

    def load(group, child, xx):
        return pltpu.make_async_copy(
            vectors_hbm.at[child, pl.ds(group * OWNERS, OWNERS), xx],
            vectors.at[group, child, xx],
            load_sem.at[group, child],
        )

    def wait_all(ref, sem):
        pltpu.make_async_copy(ref, ref, sem).wait()

    def wait_loads(group, child):
        wait_all(vectors.at[group, child], load_sem.at[group, child])

    def start_loads(group, child):
        for xx in range(NX):
            load(group, child, xx).start()

    start_loads(0, 0)
    for copy in small:
        copy.wait()

    half = position_ref.shape[1]
    for child in range(2):
        row = slice(child, child + 1)
        poles[child, 0] = jnp.broadcast_to(position_ref[row, :].astype(jnp.float32), (8, half))
        poles[child, 1] = jnp.broadcast_to(fraction_ref[row, :], (8, half))
        poles[child, 2] = jnp.broadcast_to(
            keep_ref[row, :].astype(jnp.float32) * weight_ref[row, :], (8, half)
        )
    for block in range(4):
        lanes = slice(block * 128, block * 128 + 128)
        roots[0, block * 16 : block * 16 + 16] = jnp.broadcast_to(
            root_ref[:, lanes].astype(jnp.float32), (128, 128)
        ).T.reshape(16, 8, 128)
        roots[1, block * 16 : block * 16 + 16] = jnp.broadcast_to(
            offset_ref[:, lanes], (128, 128)
        ).T.reshape(16, 8, 128)

    squares[...] = jnp.zeros_like(squares)

    def make_panel(child, side, start, stop):
        def body(step, carry):
            first = side * 32 + step * 4
            root_rows = roots[0, pl.ds(first, 4)]
            offset_rows = roots[1, pl.ds(first, 4)]
            total = jnp.zeros((4, 8, 128), jnp.float32)
            for block in range(half // 128):
                lanes = slice(block * 128, block * 128 + 128)
                spacing = (poles[child, 0, :, lanes][None] - root_rows) + (
                    poles[child, 1, :, lanes][None] - offset_rows
                )
                raw = poles[child, 2, :, lanes][None] / spacing
                total = total + raw * raw
                panel[child, pl.ds(pl.multiple_of(first * 8, 32), 32), lanes] = raw.reshape(
                    32, 128
                ).astype(jnp.bfloat16)
            squares[pl.ds(first, 4)] = squares[pl.ds(first, 4)] + total
            return carry

        lax.fori_loop(start, stop, body, 0)

    def remote(src, dst, send, recv, target):
        return pltpu.make_async_remote_copy(
            src_ref=src, dst_ref=dst, send_sem=send, recv_sem=recv, device_id=target, device_id_type=MESH
        )

    def product(group, child, columns):
        return lax.dot_general(
            vectors[group, child].reshape(NX * OWNERS * 16, half),
            panel[child, columns],
            (((1,), (1,)), ((), ())),
            preferred_element_type=jnp.float32,
        ).astype(jnp.bfloat16)

    def x_copy(group, child, side, n):
        return remote(
            part.at[group, child, side, x_peers[n]],
            arrived.at[group, child, side, n],
            x_send,
            x_recv.at[child, side],
            at(z, x_peers[n]),
        )

    def send_x(group, child, side):
        for n in range(NX - 1):
            x_copy(group, child, side, n).start()

    def send_z(group, child, side, total):
        owners = pl.ds(group * OWNERS, OWNERS)
        spread[child, side, owners] = total.astype(jnp.bfloat16)
        for n in range(OWNERS):
            zz = group * OWNERS + n

            @pl.when(zz != z)
            def _(zz=zz):
                remote(
                    spread.at[child, side, zz],
                    landed.at[child, side, z],
                    z_send,
                    z_recv.at[child, side],
                    at(zz, x),
                ).start()

        @pl.when(half_z == group)
        def _():
            landed[child, side, z] = spread[child, side, z]

    def gather(group, child, side):
        total = part[group, child, side, x].astype(jnp.float32)
        wait_all(arrived.at[group, child, side], x_recv.at[child, side])
        for n in range(NX - 1):
            total = total + arrived[group, child, side, n].astype(jnp.float32)
        send_z(group, child, side, total)

    def ring_copy(child, side, d, step):
        beside = x_peers[1 + d]
        owners = pl.ds((1 - d if step == 1 else d) * 2, 2)
        return remote(
            (
                part.at[1, child, side, x_peers[0], owners],
                part.at[1, child, side, beside, owners],
                sent.at[child, side, d],
            )[step],
            ring.at[child, side, d] if step == 0 else arrived.at[1, child, side, d, owners],
            r_send,
            r_recv.at[min(step, 1), child, side],
            at(z, beside),
        )

    def send_ring(child, side, step):
        for d in range(2):
            ring_copy(child, side, d, step).start()

    def pass_ring(child, side):
        wait_all(ring.at[child, side], r_recv.at[0, child, side])
        for d in range(2):
            sent[child, side, d] = (
                part[1, child, side, x_peers[1 + d], pl.ds(d * 2, 2)].astype(jnp.float32)
                + ring[child, side, d].astype(jnp.float32)
            ).astype(jnp.bfloat16)
        send_ring(child, side, 2)

    def gather_ring(child, side):
        total = part[1, child, side, x].astype(jnp.float32)
        wait_all(arrived.at[1, child, side, pl.ds(0, 2)], r_recv.at[1, child, side])
        for d in range(2):
            total = total + arrived[1, child, side, d].astype(jnp.float32)
        send_z(1, child, side, total)

    def tx_copy(n):
        return remote(own_total, x_totals.at[n], tx_send, tx_recv, at(z, x_peers[n]))

    def tz_copy(n):
        return remote(z_own, z_totals.at[n], tz_send, tz_recv, at(z_peers[n], x))

    def loop(count):
        def run(body):
            lax.fori_loop(0, count, lambda step, carry: (body(step), carry)[1], 0)

        return run

    @loop(4)
    def _(unit):
        child, side = unit // 2, unit % 2
        make_panel(child, side, 0, 4)
        pl.when(unit == 0)(answer)
        make_panel(child, side, 4, 8)

        @pl.when(side == 0)
        def _():
            wait_loads(0, child)

        @pl.when(unit == 0)
        def _():
            start_loads(0, 1)
            start_loads(1, 0)
            start_loads(1, 1)

        columns = pl.ds(pl.multiple_of(side * WIDTH, WIDTH), WIDTH)
        part[0, child, side] = product(0, child, columns).reshape(NX, OWNERS, 16, WIDTH)

        @pl.when(jnp.logical_and(unit == 0, x != hub_x))
        def _():
            pl.semaphore_wait(x_ready, 1)

        @pl.when(unit == 3)
        def _():
            for block in range(4):
                own_total[block : block + 1] = jnp.sum(
                    squares[block * 16 : block * 16 + 16].reshape(128, 128).T, axis=0, keepdims=True
                )
            for n in range(NX - 1):
                tx_copy(n).start()

        send_x(0, child, side)

    @pl.when(z != hub_z)
    def _():
        pl.semaphore_wait(z_ready, 1)

    gather(0, 0, 0)

    @loop(2)
    def _(child):
        wait_loads(1, child)
        block = product(1, child, slice(None))
        for side in range(2):
            part[1, child, side] = block[:, side * WIDTH : side * WIDTH + WIDTH].reshape(NX, OWNERS, 16, WIDTH)
        for side in range(2):
            send_ring(child, side, 0)


        @pl.when(child == 0)
        def _():
            gather(0, 0, 1)

    @loop(4)
    def _(unit):
        send_ring(lax.div(unit, 2), lax.rem(unit, 2), 1)

    gather(0, 1, 0)
    wait_all(x_totals, tx_recv)
    z_own[...] = own_total[...] + x_totals[0] + x_totals[1] + x_totals[2]
    for n in range(NZ - 1):
        tz_copy(n).start()
    gather(0, 1, 1)

    @loop(4)
    def _(unit):
        pass_ring(lax.div(unit, 2), lax.rem(unit, 2))

    @loop(4)
    def _(unit):
        gather_ring(lax.div(unit, 2), lax.rem(unit, 2))

    total = z_own[...]
    wait_all(z_totals, tz_recv)
    for n in range(NZ - 1):
        total = total + z_totals[n]
    scale[...] = lax.rsqrt(total)

    @loop(4)
    def _(unit):
        child, side = unit // 2, unit % 2
        wait_all(landed.at[child, side, pl.ds(0, NZ - 1)], z_recv.at[child, side])
        result = landed[child, side, 0].astype(jnp.float32)
        for n in range(1, NZ):
            result = result + landed[child, side, n].astype(jnp.float32)
        for block in range(2):
            first = pl.multiple_of(side * WIDTH + block * 128, 128)
            out_ref[child, :, pl.ds(first, 128)] = (
                result[:, block * 128 : block * 128 + 128] * scale[pl.ds(side * 2 + block, 1)]
            ).astype(jnp.bfloat16)

    wait_all(arrived.at[0], x_send)
    wait_all(part.at[1, :, :, pl.ds(0, 3)], r_send)
    wait_all(landed.at[:, :, pl.ds(0, NZ - 1)], z_send)
    wait_all(x_totals, tx_send)
    wait_all(z_totals, tz_send)


def local(child_vectors, merge_position, pole_frac, weights, retained, root_index, root_offset):
    children, rows, half = child_vectors.shape
    cols = root_index.shape[0]
    bf16, f32 = jnp.bfloat16, jnp.float32
    dma = pltpu.SemaphoreType.DMA
    sides = cols // WIDTH
    return pl.pallas_call(
        kernel,
        out_shape=jax.ShapeDtypeStruct((children, 16, cols), bf16),
        in_specs=[pl.BlockSpec(memory_space=pltpu.HBM)] * 7,
        out_specs=pl.BlockSpec(memory_space=pltpu.VMEM),
        scratch_shapes=[
            pltpu.VMEM((children, half), jnp.int32),
            pltpu.VMEM((children, half), f32),
            pltpu.VMEM((children, half), f32),
            pltpu.VMEM((children, half), jnp.int32),
            pltpu.VMEM((1, cols), jnp.int32),
            pltpu.VMEM((1, cols), f32),
            pltpu.VMEM((2, children, NX, OWNERS, 16, half), bf16),
            pltpu.VMEM((children, cols, half), bf16),
            pltpu.VMEM((children, 3, 8, half), f32),
            pltpu.VMEM((2, cols // 8, 8, 128), f32),
            pltpu.VMEM((cols // 8, 8, 128), f32),
            pltpu.VMEM((2, children, sides, NX, OWNERS, 16, WIDTH), bf16),
            pltpu.VMEM((2, children, sides, NX - 1, OWNERS, 16, WIDTH), bf16),
            pltpu.VMEM((children, sides, 2, OWNERS // 2, 16, WIDTH), bf16),
            pltpu.VMEM((children, sides, 2, OWNERS // 2, 16, WIDTH), bf16),
            pltpu.VMEM((children, sides, NZ, 16, WIDTH), bf16),
            pltpu.VMEM((children, sides, NZ, 16, WIDTH), bf16),
            pltpu.VMEM((cols // 128, 128), f32),
            pltpu.VMEM((NX - 1, cols // 128, 128), f32),
            pltpu.VMEM((cols // 128, 128), f32),
            pltpu.VMEM((NZ - 1, cols // 128, 128), f32),
            pltpu.VMEM((cols // 128, 128), f32),
            pltpu.SemaphoreType.REGULAR,
            pltpu.SemaphoreType.REGULAR,
            dma((6,)),
            dma((2, children)),
            dma,
            dma((children, sides)),
            dma,
            dma((2, children, sides)),
            dma,
            dma((children, sides)),
            dma,
            dma,
            dma,
            dma,
        ],
        compiler_params=pltpu.CompilerParams(
            collective_id=0, has_side_effects=True, vmem_limit_bytes=24 * 2**20
        ),
        name="panel_product",
    )(
        *(
            pltpu.with_memory_space_constraint(value, pltpu.HBM)
            for value in (
                child_vectors.reshape(children, NZ, NX, 16, half),
                merge_position,
                pole_frac,
                weights,
                retained,
                root_index.reshape(1, cols),
                root_offset.reshape(1, cols),
            )
        )
    )


def solution(mesh):
    return jax.shard_map(
        local,
        mesh=mesh,
        in_specs=(
            P(None, "row", "col"),
            P(None, "col"),
            P(None, "col"),
            P(None, "col"),
            P(None, "col"),
            P(),
            P(),
        ),
        out_specs=P(None, ("row", "col"), None),
        check_vma=False,
    )
```
